32 devices in a mesh: tau: 2 (over y), aux: 16 (over z, x, core).
Axes of the slice: x: 2, y: 2, z: 4, core: 2. Of those that a mesh axis runs over, the one named last changes fastest.
Arguments:
- coefficients: bfloat16 [16384, 2048], P('aux'), may hold values from -0.125 to 0.125
- green_occ: bfloat16 [16, 2048, 2048], P('tau', 'aux'), may hold values from -6 to 6
- green_vir: bfloat16 [16, 2048, 2048], P('tau', 'aux'), may hold values from -6 to 6
- minimax: float32 [16, 16], replicated, may hold values from -1.5 to 1.5
- coulomb: float32 [512], replicated, may hold values from 0.006 to 0.04
Outputs:
- screened: float32 [16, 16384, 512], P('tau', 'aux')
The draws below stay inside these ranges and needn't reach their ends.
All inputs are finite; a program needn't handle non-finite values.
Results may differ from the reference program's by a relative error of at most 0.0078.
Values may be sent and summed in bfloat16 or wider, within the bound.
No kernel may reach another device: no remote copies, remote signals or barrier semaphores. Data moves between devices by JAX's collectives and lax.ppermute only.
A program may use at most 128 MiB of HBM per device.

```python
import math
import jax
import jax.numpy as jnp
from jax import lax

NAUX = 16384
K = 2048
PANEL = 512
NT = 16
DYSON = 4


def block_levels(key, dims, shards, least, high):
    def one(position, shards_of):
        steps = jax.random.uniform(jax.random.fold_in(jax.random.fold_in(key, 6), position), (shards_of,), jnp.float32, least / len(shards), high / len(shards))
        return jnp.repeat(jnp.exp(steps), dims[position] // shards_of).reshape((-1,) + (1,) * (len(dims) - position - 1))

    factor_of = one(*shards[0])
    for cut in shards[1:]:
        factor_of = factor_of * one(*cut)
    return factor_of


def bell_draw(rng, dims, scale, reach, pieces=(), dtype=jnp.bfloat16):
    gain = block_levels(rng, dims, pieces, -0.22, 0.18) if pieces else 1.0
    result = jax.random.normal(rng, dims, jnp.float32) * scale * gain
    return jnp.minimum(jnp.maximum(result, -reach), reach).astype(dtype)


def setup_inputs(seed: int = 0) -> dict:
    streams_of = jax.random.split(jax.random.key(seed), 6)
    return {
        "coefficients": bell_draw(streams_of[0], (NAUX, K), K ** -0.5, 0.125, ((0, 16),)),
        "green_occ": bell_draw(streams_of[1], (NT, K, K), 1.0, 6.0, ((0, 2), (1, 16))),
        "green_vir": bell_draw(streams_of[2], (NT, K, K), 1.0, 6.0, ((0, 2), (1, 16))),
        "minimax": bell_draw(streams_of[3], (NT, NT), NT ** -0.5, 1.5, (), jnp.float32),
        "coulomb": jnp.clip(jnp.exp(jax.random.uniform(streams_of[4], (PANEL,), jnp.float32, math.log(0.006), math.log(0.04))), 0.006, 0.04),
    }


def reference(coefficients, green_occ, green_vir, minimax, coulomb):
    stride = NAUX // PANEL
    panel_coef = coefficients[::stride]

    def one_time(green_pair):
        occupied, virtual = green_pair
        pair_green = (occupied.astype(jnp.float32) * virtual.astype(jnp.float32)).astype(jnp.bfloat16)
        folded = jnp.dot(pair_green, panel_coef.T, preferred_element_type=jnp.float32).astype(jnp.bfloat16)
        return jnp.dot(coefficients, folded, preferred_element_type=jnp.float32)

    chi_time = lax.map(one_time, (green_occ, green_vir))
    chi_freq = jnp.einsum("wt,tpq->wpq", minimax, chi_time, precision=lax.Precision.HIGHEST)
    coupling = chi_freq[:, ::stride, :]
    screened = chi_freq
    for sweep in range(DYSON):
        screened = chi_freq + jnp.einsum("wpq,wqr->wpr", screened * coulomb, coupling, precision=lax.Precision.HIGHEST)
    return screened
```

```python
import functools

import jax
import jax.numpy as jnp
from jax import lax
from jax.experimental import pallas as pl
from jax.experimental.pallas import tpu as pltpu
from jax.sharding import PartitionSpec as P

BF16 = jnp.bfloat16
F32 = jnp.float32
ANY = pl.BlockSpec(memory_space=pl.ANY)
NT = (((1,), (1,)), ((), ()))


def dot(a, b):
    return jnp.dot(a, b, preferred_element_type=F32)


def ring_tables(size):
    chips = size // 2
    order = [2 * z for z in range(chips // 2)] + [2 * z + 1 for z in reversed(range(chips // 2))]
    ahead = [
        (2 * order[i] + core, 2 * order[(i + 1) % chips] + core)
        for i in range(chips)
        for core in range(2)
    ]
    behind = [(b, a) for a, b in ahead]
    cores = [(i, i ^ 1) for i in range(size)]
    return ahead, behind, cores


def piece_owners(size, forward):
    chips = size // 2
    me = lax.axis_index("aux")
    chip, core = me // 2, me % 2
    level, side = chip // 2, chip % 2
    place = jnp.where(side == 0, level, chips - 1 - level)
    steps = jnp.asarray(piece_steps(chips, forward), jnp.int32)
    source = (place - steps + chips) % chips
    half = chips // 2
    owner = jnp.where(source < half, 2 * source, 2 * (chips - 1 - source) + 1)
    return jnp.concatenate([2 * owner + core, 2 * owner + (1 - core)]).astype(jnp.int32)


def piece_steps(chips, forward):
    far = chips // 2 if forward else chips - 1 - chips // 2
    return [0] + list(range(1, far + 1)) + [-s for s in range(1, chips - far)]


def ring_gather(own, size, forward):
    ahead, behind, cores = ring_tables(size)
    chips = size // 2
    far = chips // 2 if forward else chips - 1 - chips // 2
    up, down = [], []
    a = b = own
    for step in range(1, chips):
        if step <= far:
            a = lax.ppermute(a, "aux", ahead)
            up.append(a)
        if step < chips - far:
            b = lax.ppermute(b, "aux", behind)
            down.append(b)
    mine = [own] + up + down
    return mine + [lax.ppermute(m, "aux", cores) for m in mine]


def fold_kernel(count, parts, owners, product, *refs):
    pieces, outs, panel_out = refs[:count], refs[count : count + parts], refs[count + parts]
    panel, sems = refs[count + parts + 1 :]
    depth = pieces[0].shape[0]

    @pl.when(pl.program_id(0) == 0)
    def _():
        copies = []
        for i in range(count):
            offset = pl.multiple_of(owners[i] * depth, depth)
            copies.append(
                pltpu.make_async_copy(pieces[i], panel.at[pl.ds(offset, depth)], sems.at[i])
            )
        for copy in copies:
            copy.start()
        for copy in copies:
            copy.wait()
        panel_out[...] = panel[...]

    times, rows, points = product.shape
    left = product[...].reshape(times * rows, points)
    width = outs[0].shape[-1]
    for part in range(parts):
        right = panel[pl.ds(part * width, width), :]
        value = lax.dot_general(left, right, NT, preferred_element_type=F32)
        outs[part][...] = value.astype(BF16).reshape(times, rows, width)


def fold(product, pieces, owners, parts):
    times, rows, points = product.shape
    count = len(pieces)
    depth = pieces[0].shape[0]
    panel = count * depth
    width = panel // parts
    group = 2 if times % 2 == 0 else 1
    outs = [jax.ShapeDtypeStruct((times, rows, width), BF16)] * parts
    outs.append(jax.ShapeDtypeStruct((panel, points), BF16))
    return pl.pallas_call(
        functools.partial(fold_kernel, count, parts),
        out_shape=outs,
        grid_spec=pltpu.PrefetchScalarGridSpec(
            num_scalar_prefetch=1,
            grid=(times // group,),
            in_specs=[pl.BlockSpec((group, rows, points), lambda i, o: (i, 0, 0))] + [ANY] * count,
            out_specs=[pl.BlockSpec((group, rows, width), lambda i, o: (i, 0, 0))] * parts
            + [pl.BlockSpec((panel, points), lambda i, o: (0, 0))],
            scratch_shapes=[
                pltpu.VMEM((panel, points), BF16),
                pltpu.SemaphoreType.DMA((count,)),
            ],
        ),
        compiler_params=pltpu.CompilerParams(dimension_semantics=("arbitrary",)),
        name="fold",
    )(owners, product, *pieces)


def mix_kernel(groups, parts, place, weights, *refs):
    folded, outs = refs[:groups], refs[groups:]
    times, rows, width = folded[0].shape
    count = times * groups
    each = outs[0].shape[0]
    base = place[0] * (each * parts)
    strip, lanes = 16, 128

    def body(i, carry):
        at = pl.ds(pl.multiple_of(i * strip, strip), strip)
        for lane in range(0, width, lanes):
            cut = slice(lane, lane + lanes)
            values = [folded[g][t, at, cut].astype(F32) for g in range(groups) for t in range(times)]
            for w in range(each * parts):
                total = None
                for g in range(groups):
                    first = ((place[0] + g) % groups) * times
                    for t in range(times):
                        term = weights[base + w, first + t] * values[g * times + t]
                        total = term if total is None else total + term
                outs[w // each][w % each, at, cut] = total.astype(BF16)
        return carry

    lax.fori_loop(0, rows // strip, body, 0)


def mix(folded, minimax, place, parts):
    times, rows, width = folded[0].shape
    groups = len(folded)
    each = minimax.shape[0] // groups // parts
    return pl.pallas_call(
        functools.partial(mix_kernel, groups, parts),
        out_shape=[jax.ShapeDtypeStruct((each, rows, width), BF16)] * parts,
        in_specs=[pl.BlockSpec(memory_space=pltpu.SMEM)] * 2
        + [pl.BlockSpec(memory_space=pltpu.VMEM)] * groups,
        out_specs=[pl.BlockSpec(memory_space=pltpu.VMEM)] * parts,
        name="mix",
    )(place, minimax, *folded)


def fetch(owners, pieces, slots, sems, index, slot):
    depth = pieces[0].shape[1]
    copies = []
    for i, piece in enumerate(pieces):
        offset = pl.multiple_of(owners[i] * depth, depth)
        copies.append(
            pltpu.make_async_copy(
                piece.at[index], slots.at[slot, pl.ds(offset, depth)], sems.at[slot, i]
            )
        )
    return copies


def gathered(owners, pieces, slots, sems):
    step, steps = pl.program_id(0), pl.num_programs(0)
    slot = lax.rem(step, 2)

    @pl.when(step == 0)
    def _():
        for copy in fetch(owners, pieces, slots, sems, 0, 0):
            copy.start()

    for copy in fetch(owners, pieces, slots, sems, step, slot):
        copy.wait()

    @pl.when(step + 1 < steps)
    def _():
        for copy in fetch(owners, pieces, slots, sems, step + 1, 1 - slot):
            copy.start()

    return slots[slot]


def chi_kernel(count, owners, coef, panel, kernel, *refs):
    pieces = refs[:count]
    chi, step, slots, sems = refs[count:]
    right = gathered(owners, pieces, slots, sems)
    chi[0] = dot(coef[...], right).astype(BF16)
    step[0] = (dot(panel[...], right) * kernel[...]).astype(BF16)


def chi_first(coef, panel, kernel, pieces, owners):
    each, depth, width = pieces[0].shape
    rows, points = coef.shape
    size = panel.shape[0]
    count = len(pieces)
    once = pl.Buffered(1)
    return pl.pallas_call(
        functools.partial(chi_kernel, count),
        out_shape=[
            jax.ShapeDtypeStruct((each, rows, width), BF16),
            jax.ShapeDtypeStruct((each, size, width), BF16),
        ],
        grid_spec=pltpu.PrefetchScalarGridSpec(
            num_scalar_prefetch=1,
            grid=(each,),
            in_specs=[
                pl.BlockSpec((rows, points), lambda i, o: (0, 0), pipeline_mode=once),
                pl.BlockSpec((size, points), lambda i, o: (0, 0), pipeline_mode=once),
                pl.BlockSpec((size, 1), lambda i, o: (0, 0), pipeline_mode=once),
            ]
            + [ANY] * count,
            out_specs=[
                pl.BlockSpec((1, rows, width), lambda i, o: (i, 0, 0)),
                pl.BlockSpec((1, size, width), lambda i, o: (i, 0, 0)),
            ],
            scratch_shapes=[
                pltpu.VMEM((2, points, width), BF16),
                pltpu.SemaphoreType.DMA((2, count)),
            ],
        ),
        compiler_params=pltpu.CompilerParams(dimension_semantics=("arbitrary",)),
        name="chi",
    )(owners, coef, panel, kernel, *pieces)


def dyson_kernel(count, aliased, owners, coef, panel, kernel, chi_a, step_a, *refs):
    pieces = refs[:count]
    out, slots, sems = refs[count + aliased :]
    right = gathered(owners, pieces, slots, sems)
    chi_b = dot(coef[...], right)
    step_b = (dot(panel[...], right) * kernel[...]).astype(BF16)
    one = jnp.concatenate([step_a[0], step_b], axis=1)
    two = dot(one, one)
    pair = one.astype(F32) + two
    series = (pair + dot(two.astype(BF16), pair.astype(BF16))).astype(BF16)
    width = chi_b.shape[1]
    left = jnp.concatenate([chi_a[0], chi_b.astype(BF16)], axis=1)
    more = dot(left, series)
    out[0, :, :width] = chi_a[0].astype(F32) + more[:, :width]
    out[0, :, width:] = chi_b + more[:, width:]


def dyson(coef, panel, kernel, chi_a, step_a, pieces, owners, total, first, before):
    each, depth, width = pieces[0].shape
    rows, points = coef.shape
    size = panel.shape[0]
    count = len(pieces)
    once = pl.Buffered(1)
    extra = [] if before is None else [before]
    return pl.pallas_call(
        functools.partial(dyson_kernel, count, len(extra)),
        out_shape=jax.ShapeDtypeStruct((total, rows, size), F32),
        grid_spec=pltpu.PrefetchScalarGridSpec(
            num_scalar_prefetch=1,
            grid=(each,),
            in_specs=[
                pl.BlockSpec((rows, points), lambda i, o: (0, 0), pipeline_mode=once),
                pl.BlockSpec((size, points), lambda i, o: (0, 0), pipeline_mode=once),
                pl.BlockSpec((size, 1), lambda i, o: (0, 0), pipeline_mode=once),
                pl.BlockSpec((1, rows, width), lambda i, o: (i, 0, 0)),
                pl.BlockSpec((1, size, width), lambda i, o: (i, 0, 0)),
            ]
            + [ANY] * (count + len(extra)),
            out_specs=pl.BlockSpec((1, rows, size), lambda i, o: (first + i, 0, 0)),
            scratch_shapes=[
                pltpu.VMEM((2, points, width), BF16),
                pltpu.SemaphoreType.DMA((2, count)),
            ],
        ),
        input_output_aliases={} if before is None else {6 + count: 0},
        compiler_params=pltpu.CompilerParams(dimension_semantics=("arbitrary",)),
        name="dyson",
    )(owners, coef, panel, kernel, chi_a, step_a, *pieces, *extra)


def per_device(coefficients, green_occ, green_vir, minimax, coulomb):
    size, planes = lax.axis_size("aux"), lax.axis_size("tau")
    rows, points = coefficients.shape
    panel_size = coulomb.shape[0]
    stride = rows * size // panel_size
    place = lax.axis_index("tau")
    owners = {way: piece_owners(size, way) for way in (True, False)}
    kernel = coulomb[:, None]

    local = coefficients.reshape(rows // stride, stride, points)[:, 0, :]
    panel_pieces = ring_gather(local, size, True)
    product = (green_occ.astype(F32) * green_vir.astype(F32)).astype(BF16)
    parts = 2
    *folded, panel = fold(product, panel_pieces, owners[True], parts)

    freqs = minimax.shape[0] // planes
    splits = 2 if freqs % 2 == 0 else 1
    where = jnp.reshape(place, (1,)).astype(jnp.int32)
    chunks = []
    for part in range(parts):
        theirs = [
            lax.ppermute(folded[part], "tau", [((i + j) % planes, i) for i in range(planes)])
            for j in range(1, planes)
        ]
        chunks.append(mix([folded[part]] + theirs, minimax, where, splits))

    each = freqs // splits
    first = []
    for s in range(splits):
        way = s % 2 == 0
        pieces = ring_gather(chunks[0][s], size, way)
        first.append(chi_first(coefficients, panel, kernel, pieces, owners[way]))
    out = None
    for s in range(splits):
        way = s % 2 == 0
        pieces = ring_gather(chunks[1][s], size, way)
        chi_a, step_a = first[s]
        out = dyson(
            coefficients, panel, kernel, chi_a, step_a, pieces, owners[way], freqs, s * each, out
        )
    return out


def solution(mesh):
    placed = (P("aux", None), P("tau", "aux", None), P("tau", "aux", None), P(), P())
    return jax.shard_map(
        per_device, mesh=mesh, in_specs=placed, out_specs=P("tau", "aux", None), check_vma=False
    )
```

```python
import functools

import jax
import jax.numpy as jnp
from jax import lax
from jax.experimental import pallas as pl
from jax.experimental.pallas import tpu as pltpu
from jax.sharding import PartitionSpec as P

BF16 = jnp.bfloat16
F32 = jnp.float32
HBM = pl.BlockSpec(memory_space=pl.ANY)
VMEM = pl.BlockSpec(memory_space=pltpu.MemorySpace.VMEM)
NT = (((1,), (1,)), ((), ()))
MIB = 1 << 20


def room(mib):
    return pltpu.CompilerParams(vmem_limit_bytes=mib * MIB)

STRIP = 16


def dot(a, b):
    return jnp.dot(a, b, preferred_element_type=F32)


def ring_tables(size):
    chips = size // 2
    order = [2 * z for z in range(chips // 2)] + [2 * z + 1 for z in reversed(range(chips // 2))]
    ahead = [
        (2 * order[i] + core, 2 * order[(i + 1) % chips] + core)
        for i in range(chips)
        for core in range(2)
    ]
    behind = [(b, a) for a, b in ahead]
    cores = [(i, i ^ 1) for i in range(size)]
    return ahead, behind, cores


class Ring:
    def __init__(self, size, own, forward):
        self.chips = size // 2
        half = self.chips // 2
        self.far = half if forward else self.chips - 1 - half
        self.near = self.chips - 1 - self.far
        self.ahead, self.behind, self.cores = ring_tables(size)
        self.held, self.pairs = {0: own}, {}

    def swap(self, step):
        self.pairs[step] = lax.ppermute(self.held[step], "aux", self.cores)

    def go(self, step):
        way = self.ahead if step > 0 else self.behind
        before = step - 1 if step > 0 else step + 1
        self.held[step] = lax.ppermute(self.held[before], "aux", way)


def ring_steps(chips, forward):
    far = chips // 2 if forward else chips - 1 - chips // 2
    return [0] + list(range(1, far + 1)) + [-s for s in range(1, chips - far)]


def owners_of(chips, steps):
    me = lax.axis_index("aux")
    chip, core = me // 2, me % 2
    level, side = chip // 2, chip % 2
    place = jnp.where(side == 0, level, chips - 1 - level)
    source = (place - jnp.repeat(jnp.asarray(steps, jnp.int32), 2) + chips) % chips
    owner = jnp.where(source < chips // 2, 2 * source, 2 * (chips - 1 - source) + 1)
    return (2 * owner + (core + jnp.arange(2 * len(steps)) % 2) % 2).astype(jnp.int32)


def product_kernel(a, b, out):
    out[...] = (a[...].astype(F32) * b[...].astype(F32)).astype(BF16)


def pair_product(occ, vir, parts):
    times, rows, points = occ.shape
    each = times // parts
    occ, vir = (pltpu.with_memory_space_constraint(v, pltpu.HBM) for v in (occ, vir))
    outs = []
    for part in range(parts):
        spec = pl.BlockSpec((1, rows, points), lambda i, part=part: (part * each + i, 0, 0))
        outs.append(
            pl.pallas_call(
                product_kernel,
                out_shape=jax.ShapeDtypeStruct((each, rows, points), BF16),
                grid=(each,),
                in_specs=[spec, spec],
                out_specs=pl.BlockSpec((1, rows, points), lambda i: (i, 0, 0)),
                compiler_params=room(8),
                name="product",
            )(occ, vir)
        )
    return outs


def fold_kernel(halves, *refs):
    products, pieces, out = refs[:halves], refs[halves:-1], refs[-1]
    right = jnp.concatenate([p[...] for p in pieces], axis=0)
    done = 0
    for product in products:
        times, rows, points = product.shape
        left = product[...].reshape(times * rows, points)
        value = lax.dot_general(left, right, NT, preferred_element_type=F32)
        out[done : done + times] = value.astype(BF16).reshape(times, rows, right.shape[0])
        done += times


def fold(products, pieces):
    rows = products[0].shape[1]
    times = sum(p.shape[0] for p in products)
    width = sum(p.shape[0] for p in pieces)
    return pl.pallas_call(
        functools.partial(fold_kernel, len(products)),
        out_shape=jax.ShapeDtypeStruct((times, rows, width), BF16),
        in_specs=[VMEM] * (len(products) + len(pieces)),
        out_specs=VMEM,
        compiler_params=room(12),
        name="fold",
    )(*products, *pieces)


def panel_kernel(owners, row, *refs):
    pieces, panel, column = refs[:-2], refs[-2], refs[-1]
    depth = pieces[0].shape[0]
    for i, piece in enumerate(pieces):
        panel[pl.ds(pl.multiple_of(owners[i] * depth, depth), depth), :] = piece[...]
    size = row.shape[1]
    down = lax.broadcasted_iota(jnp.int32, (size, size), 0)
    across = lax.broadcasted_iota(jnp.int32, (size, size), 1)
    spread = jnp.where(down == across, jnp.broadcast_to(row[...], (size, size)), 0.0)
    column[...] = jnp.sum(spread, axis=1, keepdims=True)


def assemble(pieces, owners, coulomb):
    depth, points = pieces[0].shape
    size = depth * len(pieces)
    return pl.pallas_call(
        panel_kernel,
        out_shape=[
            jax.ShapeDtypeStruct((size, points), BF16),
            jax.ShapeDtypeStruct((size, 1), F32),
        ],
        in_specs=[pl.BlockSpec(memory_space=pltpu.SMEM)] + [VMEM] * (1 + len(pieces)),
        out_specs=[VMEM, VMEM],
        compiler_params=room(8),
        name="panel",
    )(owners, coulomb[None, :], *pieces)


def mix_weights(minimax, planes):
    place = lax.axis_index("tau")
    freqs, times = minimax.shape[0] // planes, minimax.shape[1] // planes
    tall, wide = freqs * STRIP, minimax.shape[1] * STRIP
    row, column = jnp.arange(tall), jnp.arange(wide)
    time = column // STRIP
    source = ((place + time // times) % planes) * times + time % times
    left = (row[:, None] // STRIP + place * freqs == jnp.arange(minimax.shape[0])).astype(F32)
    right = (source[None, :] == jnp.arange(minimax.shape[1])[:, None]).astype(F32)
    exact = lax.Precision.HIGHEST
    spread = jnp.dot(jnp.dot(left, minimax, precision=exact), right, precision=exact)
    spread = jnp.where(row[:, None] % STRIP == column[None, :] % STRIP, spread, 0.0)
    high = lax.reduce_precision(spread, 8, 7)
    rest = spread - high
    middle = lax.reduce_precision(rest, 8, 7)
    return jnp.concatenate([high, middle, rest - middle], axis=0).astype(BF16)


def mix_kernel(groups, parts, weights, order, *refs):
    folded, outs, total = refs[: groups * parts], refs[groups * parts : -1], refs[-1]
    times, rows, width = folded[0].shape
    tall = weights.shape[0] // 3
    freqs = tall // STRIP
    for strip in range(rows // STRIP):
        at = slice(strip * STRIP, (strip + 1) * STRIP)
        right = jnp.concatenate(
            [
                jnp.concatenate(
                    [
                        folded[g * parts + p][:, at, :].reshape(times * STRIP, width)
                        for p in range(parts)
                    ],
                    axis=1,
                )
                for g in range(groups)
            ],
            axis=0,
        )
        three = dot(weights[...], right)
        value = three[:tall] + (three[tall : 2 * tall] + three[2 * tall :])
        total[:, at, :] = value.astype(BF16).reshape(freqs, STRIP, width * parts)
    placed = dot(total[...].reshape(freqs * rows, width * parts), order[...])
    placed = placed.astype(BF16).reshape(freqs, rows, width * parts)
    first = 0
    for out in outs:
        out[...] = placed[first : first + out.shape[0]]
        first += out.shape[0]


def mix(folded, weights, order, sizes):
    times, rows, width = folded[0][0].shape
    parts = len(folded[0])
    panel = width * parts
    return pl.pallas_call(
        functools.partial(mix_kernel, len(folded), parts),
        out_shape=[jax.ShapeDtypeStruct((each, rows, panel), BF16) for each in sizes],
        in_specs=[VMEM] * (len(folded) * parts + 2),
        out_specs=[VMEM] * len(sizes),
        scratch_shapes=[pltpu.VMEM((sum(sizes), rows, panel), BF16)],
        compiler_params=room(16),
        name="mix",
    )(weights, order, *[f for g in folded for f in g])


GAIN = 2
TOKEN = jax.ShapeDtypeStruct((8, 128), F32)


def columns(ref, chip, wide):
    if len(ref.shape) == 3:
        return ref[chip]
    return ref[:, pl.ds(pl.multiple_of(chip * wide, wide), wide)]


def gain_kernel(places, fresh, owners, coef, panel, *refs):
    count = 2 * len(places)
    pieces, refs = refs[:count], refs[count:]
    before, (chi, step, slot) = refs[: len(refs) - 3], refs[len(refs) - 3 :]
    each, depth, size = pieces[0].shape
    wide = 2 * depth
    for w in range(each):
        for j, place in enumerate(places):
            even = lax.rem(owners[2 * place], 2) == 0
            mine, theirs = pieces[2 * j][w], pieces[2 * j + 1][w]
            slot[w, j * wide : j * wide + depth, :] = jnp.where(even, mine, theirs)
            slot[w, j * wide + depth : (j + 1) * wide, :] = jnp.where(even, theirs, mine)
        for left, out, old in ((panel, step, 1), (coef, chi, 0)):
            total = None if fresh else before[old][w]
            for j, place in enumerate(places):
                chip = owners[2 * place] // 2
                term = dot(columns(left, chip, wide), slot[w, j * wide : (j + 1) * wide, :])
                total = term if total is None else total + term
            out[w] = total


def gain(coef, panel, pieces, owners, places, before):
    each, depth, size = pieces[0].shape
    rows = coef.shape[-2]
    return pl.pallas_call(
        functools.partial(gain_kernel, places, not before),
        out_shape=[
            jax.ShapeDtypeStruct((each, rows, size), F32),
            jax.ShapeDtypeStruct((each, panel.shape[-2], size), F32),
        ],
        in_specs=[pl.BlockSpec(memory_space=pltpu.SMEM)] + [VMEM] * (2 + len(pieces) + len(before)),
        out_specs=[VMEM] * 2,
        scratch_shapes=[pltpu.VMEM((each, 2 * depth * len(places), size), BF16)],
        input_output_aliases={3 + len(pieces) + i: i for i in range(len(before))},
        compiler_params=room(20),
        name="gain",
    )(owners, coef, panel, *pieces, *before)


def close_kernel(first, aliased, column, chi, step, *refs):
    out, token, result, sems = refs[aliased:]
    token[...] = jnp.zeros_like(token)
    each, rows, size = chi.shape
    cuts = sems.shape[1]
    part = rows // cuts
    writes = []
    for w in range(each):
        one = step[w] * column[...]
        low = one.astype(BF16)
        two = dot(low, low)
        pair = one + two
        series = (pair + dot(two.astype(BF16), pair.astype(BF16))).astype(BF16)
        for i in range(cuts):
            cut = slice(i * part, (i + 1) * part)
            result[w, cut, :] = chi[w, cut, :] + dot(chi[w, cut, :].astype(BF16), series)
            write = pltpu.make_async_copy(result.at[w, cut], out.at[first + w, cut], sems.at[w, i])
            write.start()
            writes.append(write)
    for write in writes:
        write.wait()


def close(column, chi, step, total, first, before, mark):
    each, rows, size = chi.shape
    extra = [] if before is None else [before, mark]
    cuts = 4
    return pl.pallas_call(
        functools.partial(close_kernel, first, len(extra)),
        out_shape=[jax.ShapeDtypeStruct((total, rows, size), F32), TOKEN],
        in_specs=[VMEM] * 3 + [HBM] * len(extra),
        out_specs=[HBM, VMEM],
        scratch_shapes=[
            pltpu.VMEM((each, rows, size), F32),
            pltpu.SemaphoreType.DMA((each, cuts)),
        ],
        input_output_aliases={} if before is None else {3: 0},
        compiler_params=room(24),
        name="close",
    )(column, chi, step, *extra)


def chunk_sizes(freqs):
    return SIZES[freqs] if freqs in SIZES else [1] * freqs


SIZES = {8: [4, 4]}


def per_device(coefficients, green_occ, green_vir, minimax, coulomb):
    size, planes = lax.axis_size("aux"), lax.axis_size("tau")
    rows, points = coefficients.shape
    panel_size = coulomb.shape[0]
    depth = panel_size // size
    chips = size // 2
    freqs = minimax.shape[0] // planes
    sizes = chunk_sizes(freqs)
    shifts = [[((i + j) % planes, i) for i in range(planes)] for j in range(1, planes)]

    local = coefficients.reshape(depth, rows // depth, points)[:, 0, :]
    panel_ring = Ring(size, local, True)
    panel_ring.swap(0)
    product = pair_product(green_occ, green_vir, 2 if green_occ.shape[0] % 2 == 0 else 1)
    steps = [
        [r, -r] if r <= panel_ring.near else [r, 0] for r in range(1, panel_ring.far + 1)
    ]
    mine, theirs = [], []
    order = [s for group in steps for s in group]
    natural = jnp.repeat(owners_of(chips, order), depth) * depth + jnp.arange(panel_size) % depth
    early = {
        "weights": mix_weights(minimax, planes),
        "panel": owners_of(chips, order),
        "placing": (natural[:, None] == jnp.arange(panel_size)[None, :]).astype(BF16),
    }
    for way in (True, False):
        early[way] = owners_of(chips, ring_steps(chips, way))

    def fold_group(group):
        pieces = [p for s in group for p in (panel_ring.held[s], panel_ring.pairs[s])]
        mine.append(fold(product, pieces))
        theirs.append([lax.ppermute(mine[-1], "tau", shift) for shift in shifts])

    for number, group in enumerate(steps):
        if number:
            sync = [(panel_ring.held, s) for s in steps[number - 1]]
            if number > 1:
                sync += [(panel_ring.pairs, s) for s in steps[number - 2]]
            if mine:
                sync += [(theirs[-1], k) for k in range(len(shifts))]
            if number == 1:
                sync += [(early, key) for key in early] + [(product, 0)]
            if number == 2:
                sync += [(product, len(product) - 1)]
            together(sync)
        for step in group:
            if step:
                panel_ring.go(step)
        if number:
            for step in steps[number - 1]:
                panel_ring.swap(step)
        if number > 1:
            fold_group(steps[number - 2])
    for step in steps[-1]:
        if step:
            panel_ring.swap(step)
    for group in steps[-2:] if len(steps) > 1 else steps:
        fold_group(group)
    groups = [[m] + t for m, t in zip(mine, theirs)]
    panel_pieces = [p for s in order for p in (panel_ring.held[s], panel_ring.pairs[s])]
    panel = list(assemble(panel_pieces, early["panel"], coulomb))
    chunks = mix([list(g) for g in zip(*groups)], early["weights"], early["placing"], sizes)

    rings, ups, downs, outs, marks = [], [], [], [None], []
    for i, chunk in enumerate(chunks):
        ring = Ring(size, chunk, i % 2 == 0)
        rings.append(ring)
        ups += [(i, s) for s in range(1, ring.far + 1)]
        downs += [(i, -s) for s in range(1, ring.near + 1)]
    count = max(len(ups), len(downs))
    plan = [[m[n] for m in (ups, downs) if n < len(m)] for n in range(count)]
    points_of_chip = points // chips
    left = coefficients
    if points_of_chip % 128:
        left = jnp.swapaxes(left.reshape(rows, chips, points_of_chip), 0, 1)
        panel[0] = jnp.swapaxes(panel[0].reshape(panel_size, chips, points_of_chip), 0, 1)
    sums, summed = {}, {c: 0 for c in range(len(rings))}

    def add(c, steps):
        listed = ring_steps(chips, c % 2 == 0)
        pieces = [p for s in steps for p in (rings[c].held[s], rings[c].pairs[s])]
        places = tuple(listed.index(s) for s in steps)
        chi, step = gain(
            left, panel[0], pieces, early[c % 2 == 0], places, sums.get(c, [])
        )
        sums[c] = [chi, step]
        summed[c] += len(steps)
        if summed[c] == chips:
            outs[0], mark = close(
                panel[1], chi, step, freqs, sum(sizes[:c]), outs[0], marks[-1] if marks else None
            )
            marks.append(mark)

    landed, swapped, waiting = [], [], {c: [] for c in range(len(rings))}
    for number in range(count + 2):
        moves = plan[number] if number < count else []
        sources = [(i, s - 1 if s > 0 else s + 1) for i, s in moves]
        started = [(i, s) for i, s in sources if s == 0 and 0 not in rings[i].pairs]
        sync = [(rings[i].held, s) for i, s in dict.fromkeys(sources + landed)]
        sync += [(rings[i].pairs, s) for i, s in swapped]
        if number == 1:
            sync += [(panel, 0), (panel, 1)]
        if number < count:
            sync += [(sums[c], k) for c in sums for k in range(2) if summed[c] < chips]
            if marks and summed[len(rings) - 1] < chips:
                sync += [(marks, len(marks) - 1)]
            together(sync)
        for i, s in moves:
            rings[i].go(s)
        now = list(dict.fromkeys(started + landed))
        for i, s in now:
            rings[i].swap(s)
        for c in range(len(rings)):
            waiting[c] += [s for i, s in swapped if i == c]
            last = summed[c] + len(waiting[c]) == chips
            while len(waiting[c]) >= GAIN or (last and waiting[c]):
                add(c, waiting[c][:GAIN])
                del waiting[c][:GAIN]
        landed, swapped = moves, now
    return outs[0]


def together(sync):
    values = lax.optimization_barrier(tuple(box[key] for box, key in sync))
    for (box, key), value in zip(sync, values):
        box[key] = value


def solution(mesh):
    placed = (P("aux", None), P("tau", "aux", None), P("tau", "aux", None), P(), P())
    return jax.shard_map(
        per_device, mesh=mesh, in_specs=placed, out_specs=P("tau", "aux", None), check_vma=False
    )
```

```python
import functools

import jax
import jax.numpy as jnp
from jax import lax
from jax.experimental import pallas as pl
from jax.experimental.pallas import tpu as pltpu
from jax.sharding import PartitionSpec as P

BF16 = jnp.bfloat16
F32 = jnp.float32
HBM = pl.BlockSpec(memory_space=pl.ANY)
VMEM = pl.BlockSpec(memory_space=pltpu.MemorySpace.VMEM)
NT = (((1,), (1,)), ((), ()))
MIB = 1 << 20


def room(mib):
    return pltpu.CompilerParams(vmem_limit_bytes=mib * MIB)

STRIP = 16


def dot(a, b):
    return jnp.dot(a, b, preferred_element_type=F32)


def ring_tables(size):
    chips = size // 2
    order = [2 * z for z in range(chips // 2)] + [2 * z + 1 for z in reversed(range(chips // 2))]
    ahead = [
        (2 * order[i] + core, 2 * order[(i + 1) % chips] + core)
        for i in range(chips)
        for core in range(2)
    ]
    behind = [(b, a) for a, b in ahead]
    cores = [(i, i ^ 1) for i in range(size)]
    return ahead, behind, cores


class Ring:
    def __init__(self, size, own, forward):
        self.chips = size // 2
        half = self.chips // 2
        self.far = half if forward else self.chips - 1 - half
        self.near = self.chips - 1 - self.far
        self.ahead, self.behind, self.cores = ring_tables(size)
        self.held, self.pairs = {0: own}, {}

    def swap(self, step):
        self.pairs[step] = lax.ppermute(self.held[step], "aux", self.cores)

    def go(self, step):
        way = self.ahead if step > 0 else self.behind
        before = step - 1 if step > 0 else step + 1
        self.held[step] = lax.ppermute(self.held[before], "aux", way)


def ring_steps(chips, forward):
    far = chips // 2 if forward else chips - 1 - chips // 2
    return [0] + list(range(1, far + 1)) + [-s for s in range(1, chips - far)]


def owners_of(chips, steps):
    me = lax.axis_index("aux")
    chip, core = me // 2, me % 2
    level, side = chip // 2, chip % 2
    place = jnp.where(side == 0, level, chips - 1 - level)
    source = (place - jnp.repeat(jnp.asarray(steps, jnp.int32), 2) + chips) % chips
    owner = jnp.where(source < chips // 2, 2 * source, 2 * (chips - 1 - source) + 1)
    return (2 * owner + (core + jnp.arange(2 * len(steps)) % 2) % 2).astype(jnp.int32)


def product_kernel(a, b, out):
    out[...] = (a[...].astype(F32) * b[...].astype(F32)).astype(BF16)


def pair_product(occ, vir, parts):
    times, rows, points = occ.shape
    each = times // parts
    occ, vir = (pltpu.with_memory_space_constraint(v, pltpu.HBM) for v in (occ, vir))
    outs = []
    for part in range(parts):
        spec = pl.BlockSpec((1, rows, points), lambda i, part=part: (part * each + i, 0, 0))
        outs.append(
            pl.pallas_call(
                product_kernel,
                out_shape=jax.ShapeDtypeStruct((each, rows, points), BF16),
                grid=(each,),
                in_specs=[spec, spec],
                out_specs=pl.BlockSpec((1, rows, points), lambda i: (i, 0, 0)),
                compiler_params=room(8),
                name="product",
            )(occ, vir)
        )
    return outs


def fold_kernel(halves, *refs):
    products, pieces, out = refs[:halves], refs[halves:-1], refs[-1]
    right = jnp.concatenate([p[...] for p in pieces], axis=0)
    done = 0
    for product in products:
        times, rows, points = product.shape
        left = product[...].reshape(times * rows, points)
        value = lax.dot_general(left, right, NT, preferred_element_type=F32)
        out[done : done + times] = value.astype(BF16).reshape(times, rows, right.shape[0])
        done += times


def fold(products, pieces):
    rows = products[0].shape[1]
    times = sum(p.shape[0] for p in products)
    width = sum(p.shape[0] for p in pieces)
    return pl.pallas_call(
        functools.partial(fold_kernel, len(products)),
        out_shape=jax.ShapeDtypeStruct((times, rows, width), BF16),
        in_specs=[VMEM] * (len(products) + len(pieces)),
        out_specs=VMEM,
        compiler_params=room(12),
        name="fold",
    )(*products, *pieces)


def panel_kernel(owners, row, *refs):
    pieces, panel, column = refs[:-2], refs[-2], refs[-1]
    depth = pieces[0].shape[0]
    for i, piece in enumerate(pieces):
        panel[pl.ds(pl.multiple_of(owners[i] * depth, depth), depth), :] = piece[...]
    size = row.shape[1]
    down = lax.broadcasted_iota(jnp.int32, (size, size), 0)
    across = lax.broadcasted_iota(jnp.int32, (size, size), 1)
    spread = jnp.where(down == across, jnp.broadcast_to(row[...], (size, size)), 0.0)
    column[...] = jnp.sum(spread, axis=1, keepdims=True)


def assemble(pieces, owners, coulomb):
    depth, points = pieces[0].shape
    size = depth * len(pieces)
    return pl.pallas_call(
        panel_kernel,
        out_shape=[
            jax.ShapeDtypeStruct((size, points), BF16),
            jax.ShapeDtypeStruct((size, 1), F32),
        ],
        in_specs=[pl.BlockSpec(memory_space=pltpu.SMEM)] + [VMEM] * (1 + len(pieces)),
        out_specs=[VMEM, VMEM],
        compiler_params=room(8),
        name="panel",
    )(owners, coulomb[None, :], *pieces)


def mix_weights(minimax, planes):
    place = lax.axis_index("tau")
    freqs, times = minimax.shape[0] // planes, minimax.shape[1] // planes
    tall, wide = freqs * STRIP, minimax.shape[1] * STRIP
    row, column = jnp.arange(tall), jnp.arange(wide)
    time = column // STRIP
    source = ((place + time // times) % planes) * times + time % times
    left = (row[:, None] // STRIP + place * freqs == jnp.arange(minimax.shape[0])).astype(F32)
    right = (source[None, :] == jnp.arange(minimax.shape[1])[:, None]).astype(F32)
    exact = lax.Precision.HIGHEST
    spread = jnp.dot(jnp.dot(left, minimax, precision=exact), right, precision=exact)
    spread = jnp.where(row[:, None] % STRIP == column[None, :] % STRIP, spread, 0.0)
    high = lax.reduce_precision(spread, 8, 7)
    rest = spread - high
    middle = lax.reduce_precision(rest, 8, 7)
    return jnp.concatenate([high, middle, rest - middle], axis=0).astype(BF16)


def mix_kernel(groups, parts, weights, order, *refs):
    folded, outs, total = refs[: groups * parts], refs[groups * parts : -1], refs[-1]
    times, rows, width = folded[0].shape
    tall = weights.shape[0] // 3
    freqs = tall // STRIP
    for strip in range(rows // STRIP):
        at = slice(strip * STRIP, (strip + 1) * STRIP)
        right = jnp.concatenate(
            [
                jnp.concatenate(
                    [
                        folded[g * parts + p][:, at, :].reshape(times * STRIP, width)
                        for p in range(parts)
                    ],
                    axis=1,
                )
                for g in range(groups)
            ],
            axis=0,
        )
        three = dot(weights[...], right)
        value = three[:tall] + (three[tall : 2 * tall] + three[2 * tall :])
        total[:, at, :] = value.astype(BF16).reshape(freqs, STRIP, width * parts)
    placed = dot(total[...].reshape(freqs * rows, width * parts), order[...])
    placed = placed.astype(BF16).reshape(freqs, rows, width * parts)
    first = 0
    for out in outs:
        out[...] = placed[first : first + out.shape[0]]
        first += out.shape[0]


def mix(folded, weights, order, sizes):
    times, rows, width = folded[0][0].shape
    parts = len(folded[0])
    panel = width * parts
    return pl.pallas_call(
        functools.partial(mix_kernel, len(folded), parts),
        out_shape=[jax.ShapeDtypeStruct((each, rows, panel), BF16) for each in sizes],
        in_specs=[VMEM] * (len(folded) * parts + 2),
        out_specs=[VMEM] * len(sizes),
        scratch_shapes=[pltpu.VMEM((sum(sizes), rows, panel), BF16)],
        compiler_params=room(16),
        name="mix",
    )(weights, order, *[f for g in folded for f in g])


GAIN = 2
TOKEN = jax.ShapeDtypeStruct((8, 128), F32)


def columns(ref, chip, wide):
    if len(ref.shape) == 3:
        return ref[chip]
    return ref[:, pl.ds(pl.multiple_of(chip * wide, wide), wide)]


def gain_kernel(places, fresh, owners, coef, panel, *refs):
    count = 2 * len(places)
    pieces, refs = refs[:count], refs[count:]
    before, (chi, step, slots) = refs[: len(refs) - 3], refs[len(refs) - 3 :]
    each, depth, size = pieces[0].shape
    wide = 2 * depth

    def one_frequency(w, carry):
        slot = slots.at[w]
        for j, place in enumerate(places):
            even = lax.rem(owners[2 * place], 2) == 0
            mine, theirs = pieces[2 * j][w], pieces[2 * j + 1][w]
            slot[j * wide : j * wide + depth, :] = jnp.where(even, mine, theirs)
            slot[j * wide + depth : (j + 1) * wide, :] = jnp.where(even, theirs, mine)
        for left, out, old in ((panel, step, 1), (coef, chi, 0)):
            total = None if fresh else before[old][w]
            for j, place in enumerate(places):
                chip = owners[2 * place] // 2
                term = dot(columns(left, chip, wide), slot[j * wide : (j + 1) * wide, :])
                total = term if total is None else total + term
            out[w] = total
        return carry

    lax.fori_loop(0, each, one_frequency, 0)


def gain(coef, panel, pieces, owners, places, before):
    each, depth, size = pieces[0].shape
    rows = coef.shape[-2]
    return pl.pallas_call(
        functools.partial(gain_kernel, places, not before),
        out_shape=[
            jax.ShapeDtypeStruct((each, rows, size), F32),
            jax.ShapeDtypeStruct((each, panel.shape[-2], size), F32),
        ],
        in_specs=[pl.BlockSpec(memory_space=pltpu.SMEM)] + [VMEM] * (2 + len(pieces) + len(before)),
        out_specs=[VMEM] * 2,
        scratch_shapes=[pltpu.VMEM((each, 2 * depth * len(places), size), BF16)],
        input_output_aliases={3 + len(pieces) + i: i for i in range(len(before))},
        compiler_params=room(20),
        name="gain",
    )(owners, coef, panel, *pieces, *before)


def close_kernel(first, aliased, column, chi, step, *refs):
    out, token, result, sems = refs[aliased:]
    token[...] = jnp.zeros_like(token)
    each, rows, size = chi.shape
    cuts = sems.shape[1]
    part = rows // cuts

    def write(w, i):
        cut = slice(i * part, (i + 1) * part)
        return pltpu.make_async_copy(result.at[w, cut], out.at[first + w, cut], sems.at[w, i])

    def one_frequency(w, carry):
        one = step[w] * column[...]
        low = one.astype(BF16)
        two = dot(low, low)
        pair = one + two
        series = (pair + dot(two.astype(BF16), pair.astype(BF16))).astype(BF16)
        for i in range(cuts):
            cut = slice(i * part, (i + 1) * part)
            value = chi[w, cut, :]
            result[w, cut, :] = value + dot(value.astype(BF16), series)
            write(w, i).start()
        return carry

    lax.fori_loop(0, each, one_frequency, 0)
    for w in range(each):
        for i in range(cuts):
            write(w, i).wait()


def close(column, chi, step, total, first, before, mark):
    each, rows, size = chi.shape
    extra = [] if before is None else [before, mark]
    cuts = 4
    return pl.pallas_call(
        functools.partial(close_kernel, first, len(extra)),
        out_shape=[jax.ShapeDtypeStruct((total, rows, size), F32), TOKEN],
        in_specs=[VMEM] * 3 + [HBM] * len(extra),
        out_specs=[HBM, VMEM],
        scratch_shapes=[
            pltpu.VMEM((each, rows, size), F32),
            pltpu.SemaphoreType.DMA((each, cuts)),
        ],
        input_output_aliases={} if before is None else {3: 0},
        compiler_params=room(24),
        name="close",
    )(column, chi, step, *extra)


def chunk_sizes(freqs):
    return SIZES[freqs] if freqs in SIZES else [1] * freqs


SIZES = {8: [4, 4]}
STREAMS = 1


def per_device(coefficients, green_occ, green_vir, minimax, coulomb):
    size, planes = lax.axis_size("aux"), lax.axis_size("tau")
    rows, points = coefficients.shape
    panel_size = coulomb.shape[0]
    depth = panel_size // size
    chips = size // 2
    freqs = minimax.shape[0] // planes
    sizes = chunk_sizes(freqs)
    shifts = [[((i + j) % planes, i) for i in range(planes)] for j in range(1, planes)]

    local = coefficients.reshape(depth, rows // depth, points)[:, 0, :]
    panel_ring = Ring(size, local, True)
    panel_ring.swap(0)
    product = pair_product(green_occ, green_vir, 2 if green_occ.shape[0] % 2 == 0 else 1)
    steps = [
        [r, -r] if r <= panel_ring.near else [r, 0] for r in range(1, panel_ring.far + 1)
    ]
    mine, theirs = [], []
    order = [s for group in steps for s in group]
    natural = jnp.repeat(owners_of(chips, order), depth) * depth + jnp.arange(panel_size) % depth
    early = {
        "weights": mix_weights(minimax, planes),
        "panel": owners_of(chips, order),
        "placing": (natural[:, None] == jnp.arange(panel_size)[None, :]).astype(BF16),
    }
    for way in (True, False):
        early[way] = owners_of(chips, ring_steps(chips, way))

    def fold_group(group):
        pieces = [p for s in group for p in (panel_ring.held[s], panel_ring.pairs[s])]
        if len(mine) > 1:
            together([(theirs[len(mine) - 2], k) for k in range(len(shifts))] + [(product, 0)])
        mine.append(fold(product, pieces))
        theirs.append([lax.ppermute(mine[-1], "tau", shift) for shift in shifts])

    for number in range(len(steps) + 1):
        group = steps[number] if number < len(steps) else []
        if number and group:
            sync = [(panel_ring.held, s) for s in steps[number - 1]]
            if number == 1:
                sync += [(early, key) for key in early] + [(product, 0)]
            if number == 2:
                sync += [(product, len(product) - 1)]
            if mine:
                sync += [(mine, len(mine) - 1)]
            together(sync)
        for step in group:
            if step:
                panel_ring.go(step)
        if number:
            for step in steps[number - 1]:
                if step:
                    panel_ring.swap(step)
            fold_group(steps[number - 1])
    groups = [[m] + t for m, t in zip(mine, theirs)]
    panel_pieces = [p for s in order for p in (panel_ring.held[s], panel_ring.pairs[s])]
    panel = list(assemble(panel_pieces, early["panel"], coulomb))
    chunks = mix([list(g) for g in zip(*groups)], early["weights"], early["placing"], sizes)

    rings, outs, marks = [], [None], []
    lanes = min(STREAMS, len(chunks))
    ups, downs = [[] for _ in range(lanes)], [[] for _ in range(lanes)]
    ways = {}
    for i, chunk in enumerate(chunks):
        lane = i % lanes
        ways[i] = (i // lanes + lane) % 2 == 0
        ring = Ring(size, chunk, ways[i])
        rings.append(ring)
        ups[lane] += [(i, s) for s in range(1, ring.far + 1)]
        downs[lane] += [(i, -s) for s in range(1, ring.near + 1)]
    plan = []
    for n in range(max(len(m) for m in ups + downs)):
        for lane in range(lanes):
            moves = [m[lane][n] for m in (ups, downs) if n < len(m[lane])]
            plan.append(moves)
    count = len(plan)
    points_of_chip = points // chips
    left = coefficients
    if points_of_chip % 128:
        left = jnp.swapaxes(left.reshape(rows, chips, points_of_chip), 0, 1)
        panel[0] = jnp.swapaxes(panel[0].reshape(panel_size, chips, points_of_chip), 0, 1)
    sums, summed = {}, {c: 0 for c in range(len(rings))}

    def add(c, steps):
        listed = ring_steps(chips, ways[c])
        pieces = [p for s in steps for p in (rings[c].held[s], rings[c].pairs[s])]
        places = tuple(listed.index(s) for s in steps)
        chi, step = gain(
            left, panel[0], pieces, early[ways[c]], places, sums.get(c, [])
        )
        sums[c] = [chi, step]
        summed[c] += len(steps)
        if summed[c] == chips:
            outs[0], mark = close(
                panel[1], chi, step, freqs, sum(sizes[:c]), outs[0], marks[-1] if marks else None
            )
            marks.append(mark)

    waiting, swapped = {c: [] for c in range(len(rings))}, []

    def add_waiting():
        for c in range(len(rings)):
            last = summed[c] + len(waiting[c]) == chips
            while len(waiting[c]) >= GAIN or (last and waiting[c]):
                add(c, waiting[c][:GAIN])
                del waiting[c][:GAIN]

    for number in range(count + 1):
        moves = plan[number] if number < count else []
        landed = plan[number - 1] if number else []
        sources = [(i, s - 1 if s > 0 else s + 1) for i, s in moves]
        started = [(i, s) for i, s in dict.fromkeys(sources) if s == 0 and not rings[i].pairs]
        sync = [(rings[i].held, s) for i, s in dict.fromkeys(sources + landed)]
        sync += [(rings[i].pairs, s) for i, s in swapped]
        if number == 1:
            sync += [(panel, 0), (panel, 1)]
        sync += [(sums[c], k) for c in sums for k in range(2) if summed[c] < chips]
        if marks and summed[len(rings) - 1] < chips:
            sync += [(marks, len(marks) - 1)]
        if number < count:
            together(sync)
        for i, s in moves:
            rings[i].go(s)
        before = dict(summed)
        add_waiting()
        now = list(dict.fromkeys(started + landed))
        grown = [c for c in sums if before[c] < summed[c] < chips]
        if grown and moves:
            together([(rings[i].held, s) for i, s in now] + [(sums[c], k) for c in grown for k in range(2)])
        for i, s in now:
            rings[i].swap(s)
            waiting[i].append(s)
        swapped = now
        if number >= count - 1:
            swapped = []
            add_waiting()
    return outs[0]


def together(sync):
    values = lax.optimization_barrier(tuple(box[key] for box, key in sync))
    for (box, key), value in zip(sync, values):
        box[key] = value


def solution(mesh):
    placed = (P("aux", None), P("tau", "aux", None), P("tau", "aux", None), P(), P())
    return jax.shard_map(
        per_device, mesh=mesh, in_specs=placed, out_specs=P("tau", "aux", None), check_vma=False
    )
```

```python
import functools

import jax
import jax.numpy as jnp
from jax import lax
from jax.experimental import pallas as pl
from jax.experimental.pallas import tpu as pltpu
from jax.sharding import PartitionSpec as P

BF16 = jnp.bfloat16
F32 = jnp.float32
HBM = pl.BlockSpec(memory_space=pl.ANY)
VMEM = pl.BlockSpec(memory_space=pltpu.MemorySpace.VMEM)
NT = (((1,), (1,)), ((), ()))
MIB = 1 << 20


def room(mib):
    return pltpu.CompilerParams(vmem_limit_bytes=mib * MIB)


STRIP = 16


def dot(a, b):
    return jnp.dot(a, b, preferred_element_type=F32)


def ring_tables(size):
    chips = size // 2
    order = [2 * z for z in range(chips // 2)] + [2 * z + 1 for z in reversed(range(chips // 2))]
    ahead = [
        (2 * order[i] + core, 2 * order[(i + 1) % chips] + core)
        for i in range(chips)
        for core in range(2)
    ]
    behind = [(b, a) for a, b in ahead]
    cores = [(i, i ^ 1) for i in range(size)]
    return ahead, behind, cores


class Ring:
    def __init__(self, size, own, forward):
        self.chips = size // 2
        half = self.chips // 2
        self.far = half if forward else self.chips - 1 - half
        self.near = self.chips - 1 - self.far
        self.ahead, self.behind, self.cores = ring_tables(size)
        self.held, self.pairs = {0: own}, {}

    def swap(self, step):
        self.pairs[step] = lax.ppermute(self.held[step], "aux", self.cores)

    def go(self, step):
        way = self.ahead if step > 0 else self.behind
        before = step - 1 if step > 0 else step + 1
        self.held[step] = lax.ppermute(self.held[before], "aux", way)


def ring_steps(chips, forward):
    far = chips // 2 if forward else chips - 1 - chips // 2
    return [0] + list(range(1, far + 1)) + [-s for s in range(1, chips - far)]


def owners_of(chips, steps):
    me = lax.axis_index("aux")
    chip, core = me // 2, me % 2
    level, side = chip // 2, chip % 2
    place = jnp.where(side == 0, level, chips - 1 - level)
    source = (place - jnp.repeat(jnp.asarray(steps, jnp.int32), 2) + chips) % chips
    owner = jnp.where(source < chips // 2, 2 * source, 2 * (chips - 1 - source) + 1)
    return (2 * owner + (core + jnp.arange(2 * len(steps)) % 2) % 2).astype(jnp.int32)


def product_kernel(a, b, out):
    out[...] = (a[...].astype(F32) * b[...].astype(F32)).astype(BF16)


def pair_product(occ, vir, parts):
    times, rows, points = occ.shape
    each = times // parts
    occ, vir = (pltpu.with_memory_space_constraint(v, pltpu.HBM) for v in (occ, vir))
    outs = []
    for part in range(parts):
        spec = pl.BlockSpec((1, rows, points), lambda i, part=part: (part * each + i, 0, 0))
        outs.append(
            pl.pallas_call(
                product_kernel,
                out_shape=jax.ShapeDtypeStruct((each, rows, points), BF16),
                grid=(each,),
                in_specs=[spec, spec],
                out_specs=pl.BlockSpec((1, rows, points), lambda i: (i, 0, 0)),
                compiler_params=room(8),
                name="product",
            )(occ, vir)
        )
    return outs


def fold_kernel(halves, *refs):
    products, pieces, out = refs[:halves], refs[halves:-1], refs[-1]
    right = jnp.concatenate([p[...] for p in pieces], axis=0)
    done = 0
    for product in products:
        times, rows, points = product.shape
        left = product[...].reshape(times * rows, points)
        value = lax.dot_general(left, right, NT, preferred_element_type=F32)
        out[done : done + times] = value.astype(BF16).reshape(times, rows, right.shape[0])
        done += times


def fold(products, pieces):
    rows = products[0].shape[1]
    times = sum(p.shape[0] for p in products)
    width = sum(p.shape[0] for p in pieces)
    return pl.pallas_call(
        functools.partial(fold_kernel, len(products)),
        out_shape=jax.ShapeDtypeStruct((times, rows, width), BF16),
        in_specs=[VMEM] * (len(products) + len(pieces)),
        out_specs=VMEM,
        compiler_params=room(12),
        name="fold",
    )(*products, *pieces)


def panel_kernel(owners, row, *refs):
    pieces, panel, column = refs[:-2], refs[-2], refs[-1]
    depth = pieces[0].shape[0]
    for i, piece in enumerate(pieces):
        panel[pl.ds(pl.multiple_of(owners[i] * depth, depth), depth), :] = piece[...]
    size = row.shape[1]
    down = lax.broadcasted_iota(jnp.int32, (size, size), 0)
    across = lax.broadcasted_iota(jnp.int32, (size, size), 1)
    spread = jnp.where(down == across, jnp.broadcast_to(row[...], (size, size)), 0.0)
    column[...] = jnp.sum(spread, axis=1, keepdims=True)


def assemble(pieces, owners, coulomb):
    depth, points = pieces[0].shape
    size = depth * len(pieces)
    return pl.pallas_call(
        panel_kernel,
        out_shape=[
            jax.ShapeDtypeStruct((size, points), BF16),
            jax.ShapeDtypeStruct((size, 1), F32),
        ],
        in_specs=[pl.BlockSpec(memory_space=pltpu.SMEM)] + [VMEM] * (1 + len(pieces)),
        out_specs=[VMEM, VMEM],
        compiler_params=room(8),
        name="panel",
    )(owners, coulomb[None, :], *pieces)


def mix_weights(minimax, planes):
    place = lax.axis_index("tau")
    freqs, times = minimax.shape[0] // planes, minimax.shape[1] // planes
    tall, wide = freqs * STRIP, minimax.shape[1] * STRIP
    row, column = jnp.arange(tall), jnp.arange(wide)
    time = column // STRIP
    source = ((place + time // times) % planes) * times + time % times
    left = (row[:, None] // STRIP + place * freqs == jnp.arange(minimax.shape[0])).astype(F32)
    right = (source[None, :] == jnp.arange(minimax.shape[1])[:, None]).astype(F32)
    exact = lax.Precision.HIGHEST
    spread = jnp.dot(jnp.dot(left, minimax, precision=exact), right, precision=exact)
    spread = jnp.where(row[:, None] % STRIP == column[None, :] % STRIP, spread, 0.0)
    high = lax.reduce_precision(spread, 8, 7)
    rest = spread - high
    middle = lax.reduce_precision(rest, 8, 7)
    return jnp.concatenate([high, middle, rest - middle], axis=0).astype(BF16)


def mix_kernel(groups, parts, weights, order, *refs):
    folded, outs, total = refs[: groups * parts], refs[groups * parts : -1], refs[-1]
    times, rows, width = folded[0].shape
    tall = weights.shape[0] // 3
    freqs = tall // STRIP
    for strip in range(rows // STRIP):
        at = slice(strip * STRIP, (strip + 1) * STRIP)
        right = jnp.concatenate(
            [
                jnp.concatenate(
                    [
                        folded[g * parts + p][:, at, :].reshape(times * STRIP, width)
                        for p in range(parts)
                    ],
                    axis=1,
                )
                for g in range(groups)
            ],
            axis=0,
        )
        three = dot(weights[...], right)
        value = three[:tall] + (three[tall : 2 * tall] + three[2 * tall :])
        total[:, at, :] = value.astype(BF16).reshape(freqs, STRIP, width * parts)
    placed = dot(total[...].reshape(freqs * rows, width * parts), order[...])
    placed = placed.astype(BF16).reshape(freqs, rows, width * parts)
    first = 0
    for out in outs:
        out[...] = placed[first : first + out.shape[0]]
        first += out.shape[0]


def mix(folded, weights, order, sizes):
    _, rows, width = folded[0][0].shape
    parts = len(folded[0])
    panel = width * parts
    return pl.pallas_call(
        functools.partial(mix_kernel, len(folded), parts),
        out_shape=[jax.ShapeDtypeStruct((each, rows, panel), BF16) for each in sizes],
        in_specs=[VMEM] * (len(folded) * parts + 2),
        out_specs=[VMEM] * len(sizes),
        scratch_shapes=[pltpu.VMEM((sum(sizes), rows, panel), BF16)],
        compiler_params=room(16),
        name="mix",
    )(weights, order, *[f for g in folded for f in g])


LEAST = 3
GAIN_ROOM, CLOSE_ROOM = 12, 18
TOKEN = jax.ShapeDtypeStruct((8, 128), F32)


def columns(ref, owner, depth):
    if len(ref.shape) == 3:
        return ref[owner]
    return ref[:, pl.ds(pl.multiple_of(owner * depth, depth), depth)]


def gain_kernel(places, fresh, owners, coef, panel, *refs):
    count = len(places)
    pieces, refs = refs[:count], refs[count:]
    before, (chi, step, slots) = refs[: len(refs) - 3], refs[len(refs) - 3 :]
    each, depth, _ = pieces[0].shape

    def one_frequency(w, carry):
        for j, piece in enumerate(pieces):
            slots[w, j * depth : (j + 1) * depth, :] = piece[w]
        for left, out, old in ((panel, step, 1), (coef, chi, 0)):
            total = None if fresh else before[old][w]
            for j in range(0, count, 2):
                block = [columns(left, owners[p], depth) for p in places[j : j + 2]]
                right = slots[w, j * depth : (j + len(block)) * depth, :]
                term = dot(jnp.concatenate(block, axis=1), right)
                total = term if total is None else total + term
            out[w] = total
        return carry

    lax.fori_loop(0, each, one_frequency, 0)


def gain(coef, panel, pieces, owners, places, before):
    each, depth, size = pieces[0].shape
    rows = coef.shape[-2]
    return pl.pallas_call(
        functools.partial(gain_kernel, places, not before),
        out_shape=[
            jax.ShapeDtypeStruct((each, rows, size), F32),
            jax.ShapeDtypeStruct((each, panel.shape[-2], size), F32),
        ],
        in_specs=[pl.BlockSpec(memory_space=pltpu.SMEM)] + [VMEM] * (2 + len(pieces) + len(before)),
        out_specs=[VMEM] * 2,
        scratch_shapes=[pltpu.VMEM((each, depth * len(places), size), BF16)],
        input_output_aliases={3 + len(pieces) + i: i for i in range(len(before))},
        compiler_params=room(GAIN_ROOM),
        name="gain",
    )(owners, coef, panel, *pieces, *before)


def close_kernel(first, aliased, column, chi, step, *refs):
    out, token, result, sems = refs[aliased:]
    token[...] = jnp.zeros_like(token)
    each, rows, _ = chi.shape
    cuts = sems.shape[1]
    part = rows // cuts

    def write(w, i):
        cut = slice(i * part, (i + 1) * part)
        return pltpu.make_async_copy(result.at[w, cut], out.at[first + w, cut], sems.at[w, i])

    def one_frequency(w, carry):
        one = step[w] * column[...]
        low = one.astype(BF16)
        two = dot(low, low)
        pair = one + two
        series = (pair + dot(two.astype(BF16), pair.astype(BF16))).astype(BF16)
        for i in range(cuts):
            cut = slice(i * part, (i + 1) * part)
            value = chi[w, cut, :]
            result[w, cut, :] = value + dot(value.astype(BF16), series)
            write(w, i).start()
        return carry

    lax.fori_loop(0, each, one_frequency, 0)
    for w in range(each):
        for i in range(cuts):
            write(w, i).wait()


def close(column, chi, step, total, first, before, mark):
    each, rows, size = chi.shape
    extra = [] if before is None else [before, mark]
    cuts = 4
    return pl.pallas_call(
        functools.partial(close_kernel, first, len(extra)),
        out_shape=[jax.ShapeDtypeStruct((total, rows, size), F32), TOKEN],
        in_specs=[VMEM] * 3 + [HBM] * len(extra),
        out_specs=[HBM, VMEM],
        scratch_shapes=[
            pltpu.VMEM((each, rows, size), F32),
            pltpu.SemaphoreType.DMA((each, cuts)),
        ],
        input_output_aliases={} if before is None else {3: 0},
        compiler_params=room(CLOSE_ROOM),
        name="close",
    )(column, chi, step, *extra)


def chunk_sizes(freqs):
    return SIZES[freqs] if freqs in SIZES else [1] * freqs


SIZES = {8: [4, 4]}
STREAMS = 1


def per_device(coefficients, green_occ, green_vir, minimax, coulomb):
    size, planes = lax.axis_size("aux"), lax.axis_size("tau")
    rows, points = coefficients.shape
    panel_size = coulomb.shape[0]
    depth = panel_size // size
    chips = size // 2
    freqs = minimax.shape[0] // planes
    sizes = chunk_sizes(freqs)
    shifts = [[((i + j) % planes, i) for i in range(planes)] for j in range(1, planes)]

    local = coefficients.reshape(depth, rows // depth, points)[:, 0, :]
    panel_ring = Ring(size, local, True)
    panel_ring.swap(0)
    product = pair_product(green_occ, green_vir, 2 if green_occ.shape[0] % 2 == 0 else 1)
    steps = [
        [r, -r] if r <= panel_ring.near else [r, 0] for r in range(1, panel_ring.far + 1)
    ]
    mine, theirs = [], []
    order = [s for group in steps for s in group]
    natural = jnp.repeat(owners_of(chips, order), depth) * depth + jnp.arange(panel_size) % depth
    early = {
        "weights": mix_weights(minimax, planes),
        "panel": owners_of(chips, order),
        "placing": (natural[:, None] == jnp.arange(panel_size)[None, :]).astype(BF16),
    }
    for way in (True, False):
        early[way] = owners_of(chips, ring_steps(chips, way))

    def fold_group(group):
        pieces = [p for s in group for p in (panel_ring.held[s], panel_ring.pairs[s])]
        if len(mine) > 1:
            together([(theirs[len(mine) - 2], k) for k in range(len(shifts))] + [(product, 0)])
        mine.append(fold(product, pieces))
        theirs.append([lax.ppermute(mine[-1], "tau", shift) for shift in shifts])

    for number in range(len(steps) + 1):
        group = steps[number] if number < len(steps) else []
        if number and group:
            sync = [(panel_ring.held, s) for s in steps[number - 1]]
            if number == 1:
                sync += [(early, key) for key in early] + [(product, 0)]
            if number == 2:
                sync += [(product, len(product) - 1)]
            if mine:
                sync += [(mine, len(mine) - 1)]
            together(sync)
        for step in group:
            if step:
                panel_ring.go(step)
        if number:
            for step in steps[number - 1]:
                if step:
                    panel_ring.swap(step)
            fold_group(steps[number - 1])
    groups = [[m] + t for m, t in zip(mine, theirs)]
    panel_pieces = [p for s in order for p in (panel_ring.held[s], panel_ring.pairs[s])]
    panel = list(assemble(panel_pieces, early["panel"], coulomb))
    chunks = mix([list(g) for g in zip(*groups)], early["weights"], early["placing"], sizes)

    rings, outs, marks = [], [None], []
    lanes = min(STREAMS, len(chunks))
    ups, downs = [[] for _ in range(lanes)], [[] for _ in range(lanes)]
    ways = {}
    for i, chunk in enumerate(chunks):
        lane = i % lanes
        ways[i] = (i // lanes + lane) % 2 == 0
        ring = Ring(size, chunk, ways[i])
        rings.append(ring)
        ups[lane] += [(i, s) for s in range(1, ring.far + 1)]
        downs[lane] += [(i, -s) for s in range(1, ring.near + 1)]
    plan = []
    for n in range(max(len(m) for m in ups + downs)):
        for lane in range(lanes):
            moves = [m[lane][n] for m in (ups, downs) if n < len(m[lane])]
            plan.append(moves)
    count = len(plan)
    share = points // size
    left = coefficients
    if share % 128:
        left = jnp.swapaxes(left.reshape(rows, size, share), 0, 1)
        panel[0] = jnp.swapaxes(panel[0].reshape(panel_size, size, share), 0, 1)
    sums, summed = {}, {c: 0 for c in range(len(rings))}

    def add(c, units):
        listed = ring_steps(chips, ways[c])
        pieces = [(rings[c].pairs if pair else rings[c].held)[s] for s, pair in units]
        places = tuple(2 * listed.index(s) + pair for s, pair in units)
        chi, step = gain(left, panel[0], pieces, early[ways[c]], places, sums.get(c, []))
        sums[c] = [chi, step]
        summed[c] += len(units)

    def finish(c):
        outs[0], mark = close(
            panel[1], *sums[c], freqs, sum(sizes[:c]), outs[0], marks[-1] if marks else None
        )
        marks.append(mark)

    waiting, swapped, closing = {c: [] for c in range(len(rings))}, [], []

    def add_waiting(least):
        for c in range(len(rings)):
            last = summed[c] + len(waiting[c]) == size
            if waiting[c] and (last or len(waiting[c]) >= least):
                add(c, waiting[c])
                waiting[c] = []

    for number in range(count + 1):
        moves = plan[number] if number < count else []
        landed = plan[number - 1] if number else []
        sources = [(i, s - 1 if s > 0 else s + 1) for i, s in moves]
        started = [
            (i, s) for i, s in dict.fromkeys(sources) if s == 0 and 0 not in rings[i].pairs
        ]
        sync = [(rings[i].held, s) for i, s in dict.fromkeys(sources + landed)]
        sync += [(rings[i].pairs, s) for i, s in swapped]
        if number == 1:
            sync += [(panel, 0), (panel, 1)]
        sync += [(sums[c], k) for c in sums for k in range(2) if summed[c] < size or c in closing]
        if marks:
            sync += [(marks, len(marks) - 1)]
        together(sync)
        for i, s in moves:
            rings[i].go(s)
        now = list(dict.fromkeys(started + landed))
        for i, s in now:
            waiting[i].append((s, 0))
        for i, s in swapped:
            waiting[i].append((s, 1))
        before = dict(summed)
        due, closing = closing, []
        if moves:
            add_waiting(LEAST)
            for c in due:
                finish(c)
            closing = [c for c in sums if before[c] < summed[c] == size]
            grown = [c for c in sums if before[c] < summed[c]]
            if grown and LATE_SWAPS:
                together(
                    [(rings[i].held, s) for i, s in now] + [(sums[c], k) for c in grown for k in range(2)]
                )
            for i, s in now:
                rings[i].swap(s)
        else:
            for i, s in now:
                rings[i].swap(s)
            add_waiting(1)
            for c in due:
                finish(c)
        swapped = now
    for i, s in swapped:
        waiting[i].append((s, 1))
    add_waiting(1)
    for c in range(len(rings)):
        if c >= len(marks):
            finish(c)
    return outs[0]


def together(sync):
    values = lax.optimization_barrier(tuple(box[key] for box, key in sync))
    for (box, key), value in zip(sync, values):
        box[key] = value


LATE_SWAPS = False


def solution(mesh):
    placed = (P("aux", None), P("tau", "aux", None), P("tau", "aux", None), P(), P())

    return jax.shard_map(
        per_device, mesh=mesh, in_specs=placed, out_specs=P("tau", "aux", None), check_vma=False
    )
```

```python
import functools

import jax
import jax.numpy as jnp
from jax import lax
from jax.experimental import pallas as pl
from jax.experimental.pallas import tpu as pltpu
from jax.sharding import PartitionSpec as P

BF16 = jnp.bfloat16
F32 = jnp.float32
HBM = pl.BlockSpec(memory_space=pl.ANY)
VMEM = pl.BlockSpec(memory_space=pltpu.MemorySpace.VMEM)
NT = (((1,), (1,)), ((), ()))
MIB = 1 << 20


def room(mib):
    return pltpu.CompilerParams(vmem_limit_bytes=mib * MIB)


STRIP = 16


def dot(a, b):
    return jnp.dot(a, b, preferred_element_type=F32)


def ring_tables(size):
    chips = size // 2
    order = [2 * z for z in range(chips // 2)] + [2 * z + 1 for z in reversed(range(chips // 2))]
    ahead = [
        (2 * order[i] + core, 2 * order[(i + 1) % chips] + core)
        for i in range(chips)
        for core in range(2)
    ]
    behind = [(b, a) for a, b in ahead]
    cores = [(i, i ^ 1) for i in range(size)]
    return ahead, behind, cores


class Ring:
    def __init__(self, size, own, forward):
        self.chips = size // 2
        half = self.chips // 2
        self.far = half if forward else self.chips - 1 - half
        self.near = self.chips - 1 - self.far
        self.ahead, self.behind, self.cores = ring_tables(size)
        self.held, self.pairs = {0: own}, {}

    def swap(self, step):
        self.pairs[step] = lax.ppermute(self.held[step], "aux", self.cores)

    def go(self, step):
        way = self.ahead if step > 0 else self.behind
        before = step - 1 if step > 0 else step + 1
        self.held[step] = lax.ppermute(self.held[before], "aux", way)


def ring_steps(chips, forward):
    far = chips // 2 if forward else chips - 1 - chips // 2
    return [0] + list(range(1, far + 1)) + [-s for s in range(1, chips - far)]


def owners_of(chips, steps):
    me = lax.axis_index("aux")
    chip, core = me // 2, me % 2
    level, side = chip // 2, chip % 2
    place = jnp.where(side == 0, level, chips - 1 - level)
    source = (place - jnp.repeat(jnp.asarray(steps, jnp.int32), 2) + chips) % chips
    owner = jnp.where(source < chips // 2, 2 * source, 2 * (chips - 1 - source) + 1)
    return (2 * owner + (core + jnp.arange(2 * len(steps)) % 2) % 2).astype(jnp.int32)


def product_kernel(a, b, out):
    out[...] = (a[...].astype(F32) * b[...].astype(F32)).astype(BF16)


def pair_product(occ, vir, parts):
    times, rows, points = occ.shape
    each = times // parts
    occ, vir = (pltpu.with_memory_space_constraint(v, pltpu.HBM) for v in (occ, vir))
    outs = []
    for part in range(parts):
        spec = pl.BlockSpec((1, rows, points), lambda i, part=part: (part * each + i, 0, 0))
        outs.append(
            pl.pallas_call(
                product_kernel,
                out_shape=jax.ShapeDtypeStruct((each, rows, points), BF16),
                grid=(each,),
                in_specs=[spec, spec],
                out_specs=pl.BlockSpec((1, rows, points), lambda i: (i, 0, 0)),
                compiler_params=room(8),
                name="product",
            )(occ, vir)
        )
    return outs


def fold_kernel(halves, *refs):
    products, pieces, out = refs[:halves], refs[halves:-1], refs[-1]
    right = jnp.concatenate([p[...] for p in pieces], axis=0)
    done = 0
    for product in products:
        times, rows, points = product.shape
        left = product[...].reshape(times * rows, points)
        value = lax.dot_general(left, right, NT, preferred_element_type=F32)
        out[done : done + times] = value.astype(BF16).reshape(times, rows, right.shape[0])
        done += times


def fold(products, pieces):
    rows = products[0].shape[1]
    times = sum(p.shape[0] for p in products)
    width = sum(p.shape[0] for p in pieces)
    return pl.pallas_call(
        functools.partial(fold_kernel, len(products)),
        out_shape=jax.ShapeDtypeStruct((times, rows, width), BF16),
        in_specs=[VMEM] * (len(products) + len(pieces)),
        out_specs=VMEM,
        compiler_params=room(12),
        name="fold",
    )(*products, *pieces)


def panel_kernel(owners, row, *refs):
    pieces, panel, column = refs[:-2], refs[-2], refs[-1]
    depth = pieces[0].shape[0]
    for i, piece in enumerate(pieces):
        panel[pl.ds(pl.multiple_of(owners[i] * depth, depth), depth), :] = piece[...]
    size = row.shape[1]
    down = lax.broadcasted_iota(jnp.int32, (size, size), 0)
    across = lax.broadcasted_iota(jnp.int32, (size, size), 1)
    spread = jnp.where(down == across, jnp.broadcast_to(row[...], (size, size)), 0.0)
    column[...] = jnp.sum(spread, axis=1, keepdims=True)


def assemble(pieces, owners, coulomb):
    depth, points = pieces[0].shape
    size = depth * len(pieces)
    return pl.pallas_call(
        panel_kernel,
        out_shape=[
            jax.ShapeDtypeStruct((size, points), BF16),
            jax.ShapeDtypeStruct((size, 1), F32),
        ],
        in_specs=[pl.BlockSpec(memory_space=pltpu.SMEM)] + [VMEM] * (1 + len(pieces)),
        out_specs=[VMEM, VMEM],
        compiler_params=room(8),
        name="panel",
    )(owners, coulomb[None, :], *pieces)


def mix_weights(minimax, planes):
    place = lax.axis_index("tau")
    freqs, times = minimax.shape[0] // planes, minimax.shape[1] // planes
    tall, wide = freqs * STRIP, minimax.shape[1] * STRIP
    row, column = jnp.arange(tall), jnp.arange(wide)
    time = column // STRIP
    source = ((place + time // times) % planes) * times + time % times
    left = (row[:, None] // STRIP + place * freqs == jnp.arange(minimax.shape[0])).astype(F32)
    right = (source[None, :] == jnp.arange(minimax.shape[1])[:, None]).astype(F32)
    exact = lax.Precision.HIGHEST
    spread = jnp.dot(jnp.dot(left, minimax, precision=exact), right, precision=exact)
    spread = jnp.where(row[:, None] % STRIP == column[None, :] % STRIP, spread, 0.0)
    high = lax.reduce_precision(spread, 8, 7)
    rest = spread - high
    middle = lax.reduce_precision(rest, 8, 7)
    return jnp.concatenate([high, middle, rest - middle], axis=0).astype(BF16)


def mix_kernel(groups, parts, weights, order, *refs):
    folded, outs, total = refs[: groups * parts], refs[groups * parts : -1], refs[-1]
    times, rows, width = folded[0].shape
    tall = weights.shape[0] // 3
    freqs = tall // STRIP
    for strip in range(rows // STRIP):
        at = slice(strip * STRIP, (strip + 1) * STRIP)
        right = jnp.concatenate(
            [
                jnp.concatenate(
                    [
                        folded[g * parts + p][:, at, :].reshape(times * STRIP, width)
                        for p in range(parts)
                    ],
                    axis=1,
                )
                for g in range(groups)
            ],
            axis=0,
        )
        three = dot(weights[...], right)
        value = three[:tall] + (three[tall : 2 * tall] + three[2 * tall :])
        total[:, at, :] = value.astype(BF16).reshape(freqs, STRIP, width * parts)
    placed = dot(total[...].reshape(freqs * rows, width * parts), order[...])
    placed = placed.astype(BF16).reshape(freqs, rows, width * parts)
    first = 0
    for out in outs:
        out[...] = placed[first : first + out.shape[0]]
        first += out.shape[0]


def mix(folded, weights, order, sizes):
    _, rows, width = folded[0][0].shape
    parts = len(folded[0])
    panel = width * parts
    return pl.pallas_call(
        functools.partial(mix_kernel, len(folded), parts),
        out_shape=[jax.ShapeDtypeStruct((each, rows, panel), BF16) for each in sizes],
        in_specs=[VMEM] * (len(folded) * parts + 2),
        out_specs=[VMEM] * len(sizes),
        scratch_shapes=[pltpu.VMEM((sum(sizes), rows, panel), BF16)],
        compiler_params=room(16),
        name="mix",
    )(weights, order, *[f for g in folded for f in g])


LEAST = 3
GAIN_ROOM, CLOSE_ROOM = 10, 16
TOKEN = jax.ShapeDtypeStruct((8, 128), F32)


def columns(ref, owner, depth):
    if len(ref.shape) == 3:
        return ref[owner]
    return ref[:, pl.ds(pl.multiple_of(owner * depth, depth), depth)]


def gain_kernel(places, fresh, owners, coef, panel, *refs):
    count = len(places)
    pieces, refs = refs[:count], refs[count:]
    before, (chi, step, slots) = refs[: len(refs) - 3], refs[len(refs) - 3 :]
    each, depth, _ = pieces[0].shape

    def one_frequency(w, carry):
        for j, piece in enumerate(pieces):
            slots[w, j * depth : (j + 1) * depth, :] = piece[w]
        for left, out, old in ((panel, step, 1), (coef, chi, 0)):
            total = None if fresh else before[old][w]
            for j in range(0, count, 2):
                block = [columns(left, owners[p], depth) for p in places[j : j + 2]]
                right = slots[w, j * depth : (j + len(block)) * depth, :]
                term = dot(jnp.concatenate(block, axis=1), right)
                total = term if total is None else total + term
            out[w] = total
        return carry

    lax.fori_loop(0, each, one_frequency, 0)


def gain(coef, panel, pieces, owners, places, before):
    each, depth, size = pieces[0].shape
    rows = coef.shape[-2]
    return pl.pallas_call(
        functools.partial(gain_kernel, places, not before),
        out_shape=[
            jax.ShapeDtypeStruct((each, rows, size), F32),
            jax.ShapeDtypeStruct((each, panel.shape[-2], size), F32),
        ],
        in_specs=[pl.BlockSpec(memory_space=pltpu.SMEM)] + [VMEM] * (2 + len(pieces) + len(before)),
        out_specs=[VMEM] * 2,
        scratch_shapes=[pltpu.VMEM((each, depth * len(places), size), BF16)],
        input_output_aliases={3 + len(pieces) + i: i for i in range(len(before))},
        compiler_params=room(GAIN_ROOM),
        name="gain",
    )(owners, coef, panel, *pieces, *before)


def close_kernel(first, aliased, column, chi, step, *refs):
    out, token, result, sems = refs[aliased:]
    token[...] = jnp.zeros_like(token)
    each, rows, _ = chi.shape
    cuts = sems.shape[1]
    part = rows // cuts

    def write(w, i):
        cut = slice(i * part, (i + 1) * part)
        return pltpu.make_async_copy(result.at[w, cut], out.at[first + w, cut], sems.at[w, i])

    def one_frequency(w, carry):
        one = step[w] * column[...]
        low = one.astype(BF16)
        two = dot(low, low)
        pair = one + two
        series = (pair + dot(two.astype(BF16), pair.astype(BF16))).astype(BF16)
        for i in range(cuts):
            cut = slice(i * part, (i + 1) * part)
            value = chi[w, cut, :]
            result[w, cut, :] = value + dot(value.astype(BF16), series)
            write(w, i).start()
        return carry

    lax.fori_loop(0, each, one_frequency, 0)
    for w in range(each):
        for i in range(cuts):
            write(w, i).wait()


def close(column, chi, step, total, first, before, mark):
    each, rows, size = chi.shape
    extra = [] if before is None else [before, mark]
    cuts = 8
    return pl.pallas_call(
        functools.partial(close_kernel, first, len(extra)),
        out_shape=[jax.ShapeDtypeStruct((total, rows, size), F32), TOKEN],
        in_specs=[VMEM] * 3 + [HBM] * len(extra),
        out_specs=[HBM, VMEM],
        scratch_shapes=[
            pltpu.VMEM((each, rows, size), F32),
            pltpu.SemaphoreType.DMA((each, cuts)),
        ],
        input_output_aliases={} if before is None else {3: 0},
        compiler_params=room(CLOSE_ROOM),
        name="close",
    )(column, chi, step, *extra)


def chunk_sizes(freqs):
    return SIZES[freqs] if freqs in SIZES else [1] * freqs


SIZES = {8: [4, 4]}
STREAMS = 1


def per_device(coefficients, green_occ, green_vir, minimax, coulomb):
    size, planes = lax.axis_size("aux"), lax.axis_size("tau")
    rows, points = coefficients.shape
    panel_size = coulomb.shape[0]
    depth = panel_size // size
    chips = size // 2
    freqs = minimax.shape[0] // planes
    sizes = chunk_sizes(freqs)
    shifts = [[((i + j) % planes, i) for i in range(planes)] for j in range(1, planes)]

    local = coefficients.reshape(depth, rows // depth, points)[:, 0, :]
    panel_ring = Ring(size, local, True)
    panel_ring.swap(0)
    product = pair_product(green_occ, green_vir, 2 if green_occ.shape[0] % 2 == 0 else 1)
    steps = [
        [r, -r] if r <= panel_ring.near else [r, 0] for r in range(1, panel_ring.far + 1)
    ]
    mine, theirs = [], []
    order = [s for group in steps for s in group]
    natural = jnp.repeat(owners_of(chips, order), depth) * depth + jnp.arange(panel_size) % depth
    early = {
        "weights": mix_weights(minimax, planes),
        "panel": owners_of(chips, order),
        "placing": (natural[:, None] == jnp.arange(panel_size)[None, :]).astype(BF16),
    }
    for way in (True, False):
        early[way] = owners_of(chips, ring_steps(chips, way))

    def fold_group(group):
        pieces = [p for s in group for p in (panel_ring.held[s], panel_ring.pairs[s])]
        if len(mine) > 1:
            together([(theirs[len(mine) - 2], k) for k in range(len(shifts))] + [(product, 0)])
        mine.append(fold(product, pieces))
        theirs.append([lax.ppermute(mine[-1], "tau", shift) for shift in shifts])

    for number in range(len(steps) + 1):
        group = steps[number] if number < len(steps) else []
        if number and group:
            sync = [(panel_ring.held, s) for s in steps[number - 1]]
            if number == 1:
                sync += [(early, key) for key in early] + [(product, 0)]
            if number == 2:
                sync += [(product, len(product) - 1)]
            if mine:
                sync += [(mine, len(mine) - 1)]
            together(sync)
        for step in group:
            if step:
                panel_ring.go(step)
        if number:
            for step in steps[number - 1]:
                if step:
                    panel_ring.swap(step)
            fold_group(steps[number - 1])
    groups = [[m] + t for m, t in zip(mine, theirs)]
    panel_pieces = [p for s in order for p in (panel_ring.held[s], panel_ring.pairs[s])]
    panel = list(assemble(panel_pieces, early["panel"], coulomb))
    chunks = mix([list(g) for g in zip(*groups)], early["weights"], early["placing"], sizes)

    rings, outs, marks = [], [None], []
    lanes = min(STREAMS, len(chunks))
    ups, downs = [[] for _ in range(lanes)], [[] for _ in range(lanes)]
    ways = {}
    for i, chunk in enumerate(chunks):
        lane = i % lanes
        ways[i] = (i // lanes + lane) % 2 == 0
        ring = Ring(size, chunk, ways[i])
        rings.append(ring)
        ups[lane] += [(i, s) for s in range(1, ring.far + 1)]
        downs[lane] += [(i, -s) for s in range(1, ring.near + 1)]
    plan = []
    for n in range(max(len(m) for m in ups + downs)):
        for lane in range(lanes):
            moves = [m[lane][n] for m in (ups, downs) if n < len(m[lane])]
            plan.append(moves)
    count = len(plan)
    share = points // size
    left = coefficients
    if share % 128:
        left = jnp.swapaxes(left.reshape(rows, size, share), 0, 1)
        panel[0] = jnp.swapaxes(panel[0].reshape(panel_size, size, share), 0, 1)
    sums, summed = {}, {c: 0 for c in range(len(rings))}

    def add(c, units):
        listed = ring_steps(chips, ways[c])
        pieces = [(rings[c].pairs if pair else rings[c].held)[s] for s, pair in units]
        places = tuple(2 * listed.index(s) + pair for s, pair in units)
        chi, step = gain(left, panel[0], pieces, early[ways[c]], places, sums.get(c, []))
        sums[c] = [chi, step]
        summed[c] += len(units)

    def finish(c):
        outs[0], mark = close(
            panel[1], *sums[c], freqs, sum(sizes[:c]), outs[0], marks[-1] if marks else None
        )
        marks.append(mark)

    waiting, swapped = {c: [] for c in range(len(rings))}, []

    def add_waiting(least):
        ends = [c for c in waiting if waiting[c] and summed[c] + len(waiting[c]) == size]
        for c in ends if ends and least > 1 else range(len(rings)):
            if waiting[c] and (c in ends or len(waiting[c]) >= least):
                add(c, waiting[c])
                waiting[c] = []
        return ends if least > 1 else []

    for number in range(count + 1):
        moves = plan[number] if number < count else []
        landed = plan[number - 1] if number else []
        sources = [(i, s - 1 if s > 0 else s + 1) for i, s in moves]
        started = [
            (i, s) for i, s in dict.fromkeys(sources) if s == 0 and 0 not in rings[i].pairs
        ]
        sync = [(rings[i].held, s) for i, s in dict.fromkeys(sources + landed)]
        sync += [(rings[i].pairs, s) for i, s in swapped]
        if number == 1:
            sync += [(panel, 0), (panel, 1)]
        sync += [(sums[c], k) for c in sums for k in range(2) if summed[c] < size]
        if marks:
            sync += [(marks, len(marks) - 1)]
        together(sync)
        for i, s in moves:
            rings[i].go(s)
        now = list(dict.fromkeys(started + landed))
        for i, s in now:
            waiting[i].append((s, 0))
        for i, s in swapped:
            waiting[i].append((s, 1))
        before = dict(summed)
        if moves:
            for c in add_waiting(LEAST):
                finish(c)
            grown = [c for c in sums if before[c] < summed[c]]
            if grown and LATE_SWAPS:
                together(
                    [(rings[i].held, s) for i, s in now] + [(sums[c], k) for c in grown for k in range(2)]
                )
            for i, s in now:
                rings[i].swap(s)
        else:
            for i, s in now:
                rings[i].swap(s)
            add_waiting(1)
        swapped = now
    for i, s in swapped:
        waiting[i].append((s, 1))
    add_waiting(1)
    for c in range(len(rings)):
        if c >= len(marks):
            finish(c)
    return outs[0]


def together(sync):
    values = lax.optimization_barrier(tuple(box[key] for box, key in sync))
    for (box, key), value in zip(sync, values):
        box[key] = value


LATE_SWAPS = False


def solution(mesh):
    placed = (P("aux", None), P("tau", "aux", None), P("tau", "aux", None), P(), P())

    return jax.shard_map(
        per_device, mesh=mesh, in_specs=placed, out_specs=P("tau", "aux", None), check_vma=False
    )
```
